32 devices in a mesh: outer: 4 (over y, x), inner: 2 (over core), col: 4 (over z).
Axes of the slice: x: 2, y: 2, z: 4, core: 2. Of those that a mesh axis runs over, the one named last changes fastest.
Arguments:
- operator: bfloat16 [4096, 8192], P(('outer', 'inner'), 'col'), as said below
- test_matrix: bfloat16 [8192, 256], P('col'), may hold values from -6 to 6
Outputs:
- basis: float32 [4096, 256], P(('outer', 'inner'), 'col')
- factor: float32 [256, 256], replicated
The draws below stay inside these ranges and needn't reach their ends.
Inputs may be any that keep to these rules, and one draw needn't show every extreme that they name: Entries of the operator are of order 1 / sqrt(8192) times row and column scales between 0.5 and 4.
All inputs are finite; a program needn't handle non-finite values.
Results may differ from the reference program's by a relative error of at most 0.003.
Values may be sent and summed in bfloat16 or wider, within the bound.
A program may use at most 64 MiB of HBM per device.

```python
import jax
import jax.numpy as jnp
from jax import lax

N = 8192
K = 256
ROWS = 4096


def draw_operator(key, part):
    key_base = jax.random.fold_in(key, 11)
    key_rows = jax.random.fold_in(key, 12)
    key_cols = jax.random.fold_in(key, 13)
    position = jnp.arange(ROWS, dtype=jnp.float32).reshape(ROWS, 1) / ROWS
    row_scale = jnp.exp(position * jnp.log(3.0) + jax.random.uniform(key_rows, (ROWS, 1), jnp.float32, -0.25, 0.25))
    col_scale = jnp.exp(jax.random.uniform(key_cols, (1, N), jnp.float32, -0.35, 0.35))
    base = jax.random.normal(key_base, (ROWS, N), jnp.float32)
    return (base * row_scale * col_scale / jnp.sqrt(jnp.float32(N))).astype(jnp.bfloat16)


def block_scale(key, extent, shards, least, largest):
    loudness, own = 1.0, jax.random.fold_in(key, 6)
    for axis_at, parts in shards:
        draws = jnp.exp(jax.random.uniform(jax.random.fold_in(own, axis_at), (parts,), jnp.float32, least / len(shards), largest / len(shards)))
        loudness = loudness * jnp.repeat(draws, extent[axis_at] // parts).reshape([-1 if axis == axis_at else 1 for axis in range(len(extent))])
    return loudness


def scatter_about(stream_key, shape, deviation, most, shards=(), kind=jnp.bfloat16):
    factor_of = block_scale(stream_key, shape, shards, -0.22, 0.18) if shards else 1.0
    entries = jax.random.normal(stream_key, shape, jnp.float32) * deviation * factor_of
    return jnp.minimum(jnp.maximum(entries, -most), most).astype(kind)


def setup_inputs(seed: int = 0) -> dict:
    seeds = jax.random.split(jax.random.key(seed), 3)
    operator = draw_operator(jax.random.fold_in(seeds[2], 71), 0)
    test_matrix = scatter_about(seeds[1], (N, K), 1.0, 6.0, ((0, 4),))
    return dict(operator=operator, test_matrix=test_matrix)


def gram_of(matrix):
    return jnp.dot(matrix.T.astype(jnp.float32), matrix.astype(jnp.float32), precision=lax.Precision.HIGHEST, preferred_element_type=jnp.float32)

def right_solve(lower, matrix):
    return jax.scipy.linalg.solve_triangular(lower, matrix.T, lower=True).T

def reference(operator, test_matrix):
    sketch = jnp.dot(operator.astype(jnp.float32), test_matrix.astype(jnp.float32), preferred_element_type=jnp.float32).astype(jnp.bfloat16)
    total = jnp.dot(operator.T.astype(jnp.float32), sketch.astype(jnp.float32), preferred_element_type=jnp.float32)
    normal = (total * (N / ROWS)).astype(jnp.bfloat16)
    image = jnp.dot(operator.astype(jnp.float32), normal.astype(jnp.float32), preferred_element_type=jnp.float32)
    lower = jnp.linalg.cholesky(gram_of(image))
    orthonormal = right_solve(lower, image)
    root = jnp.sqrt(jnp.float32(ROWS))
    basis = orthonormal * root
    factor = lower.T / root
    return (basis, factor)
```

```python
import functools

import jax
import jax.numpy as jnp
from jax import lax
from jax.experimental import pallas as pl
from jax.experimental.pallas import tpu as pltpu
from jax.sharding import PartitionSpec as P

F32 = jnp.float32
BF16 = jnp.bfloat16
MESH = pl.DeviceIdType.MESH
HIGHEST = lax.Precision.HIGHEST
SKETCH_WIRE = F32
NORMAL_WIRE = F32
IMAGE_WIRE = F32


def power_kernel(
    sizes, ratio, a_hbm, om_hbm, gram_ref, image_ref,
    a, om, p1, w1, r1, sk, p2, w2, r2, nt, p3, w3, r3, x, gp, ra, gb, gf, im,
    load_sem, s0, v0, s1, v1, s2, v2, s3, v3, s4, v4, s5, v5, s6, v6, s7, v7, s8, v8, s9, v9,
):
    outer, inner, cols = sizes
    chips = inner // 2
    groups = outer * chips
    o, i, c = lax.axis_index("outer"), lax.axis_index("inner"), lax.axis_index("col")
    k = lax.rem(i, 2)
    other = 1 - k
    chip = lax.div(i, 2)
    r = o * chips + chip
    partner = (o, chip * 2 + other, c)

    def col_peer(s):
        return lax.rem(c + s, cols)

    def row_peer(s):
        return lax.rem(r + s, groups)

    def at_col(to, core):
        return (o, chip * 2 + core, to)

    def at_row(to):
        return (lax.div(to, chips), lax.rem(to, chips) * 2 + k, c)

    def send(src, dst, ss, rs, to):
        copy = pltpu.make_async_remote_copy(
            src_ref=src, dst_ref=dst, send_sem=ss, recv_sem=rs, device_id=to, device_id_type=MESH
        )
        copy.start()
        return copy

    load_a = pltpu.make_async_copy(a_hbm, a.at[k], load_sem.at[0])
    load_a.start()
    width = om.shape[1]
    load_om = pltpu.make_async_copy(
        om_hbm.at[:, pl.ds(pl.multiple_of(k * width, width), width)], om, load_sem.at[1]
    )
    load_om.start()

    barrier = pltpu.get_barrier_semaphore()
    peers = [partner]
    for s in range(1, cols):
        peers += [at_col(col_peer(s), k), at_col(col_peer(s), other)]
    for s in range(1, groups):
        peers.append(at_row(row_peer(s)))
    for to in peers:
        pl.semaphore_signal(barrier, inc=1, device_id=to, device_id_type=MESH)
    pl.semaphore_wait(barrier, len(peers))

    pair = send(a_hbm, a.at[k], s0, v0, partner)
    load_a.wait()
    load_om.wait()

    part = p1.shape[1] // cols
    own = pl.ds(pl.multiple_of(c * part, part), part)

    def rows_of(to):
        return pl.ds(pl.multiple_of(to * part, part), part)

    copies = []
    for turn, block in enumerate((k, other)):
        if turn == 1:
            pair.wait()
        partial = jnp.dot(a[block], om[...], preferred_element_type=F32)
        p1[block] = partial
        if SKETCH_WIRE != F32:
            w1[block] = partial.astype(SKETCH_WIRE)
        for s in range(1, cols):
            to = col_peer(s)
            n = (s - 1) * 2 + turn
            copies.append(send(
                (p1 if SKETCH_WIRE == F32 else w1).at[block, rows_of(to)],
                r1.at[s - 1, turn], s1.at[n], v1.at[n], at_col(to, k)))
    for copy in copies:
        copy.wait()
    for turn, block in enumerate((k, other)):
        total = p1[block, own]
        for s in range(1, cols):
            total = total + r1[s - 1, turn].astype(F32)
        sk[block, own] = total.astype(BF16)
    copies = []
    for s in range(1, cols):
        copies.append(send(sk.at[:, own], sk.at[:, own], s2.at[s - 1], v2.at[s - 1], at_col(col_peer(s), k)))
    for copy in copies:
        copy.wait()

    normal = None
    for block in range(2):
        st = sk[block].astype(F32).T.astype(BF16)
        term = jnp.dot(st, a[block], preferred_element_type=F32)
        normal = term if normal is None else normal + term
    lanes = p2.shape[1]
    for g in range(groups):
        p2[g] = normal[g * lanes:(g + 1) * lanes]
        if NORMAL_WIRE != F32:
            w2[g] = normal[g * lanes:(g + 1) * lanes].astype(NORMAL_WIRE)
    copies = []
    for s in range(1, groups):
        to = row_peer(s)
        copies.append(send((p2 if NORMAL_WIRE == F32 else w2).at[to], r2.at[s - 1], s3.at[s - 1], v3.at[s - 1], at_row(to)))
    for copy in copies:
        copy.wait()
    total = p2[r]
    for s in range(1, groups):
        total = total + r2[s - 1].astype(F32)
    nt[r] = (total * ratio).astype(BF16)
    copies = []
    for s in range(1, groups):
        copies.append(send(nt.at[r], nt.at[r], s4.at[s - 1], v4.at[s - 1], at_row(row_peer(s))))
    for copy in copies:
        copy.wait()
    if lanes % 16 == 0:
        whole = nt[...].reshape(groups * lanes, nt.shape[2])
    else:
        whole = jnp.concatenate([nt[g].astype(F32) for g in range(groups)], axis=0).astype(BF16)

    copies = []
    for block in range(2):
        partial = lax.dot_general(a[block], whole, (((1,), (1,)), ((), ())), preferred_element_type=F32)
        p3[block] = partial
        if IMAGE_WIRE != F32:
            w3[block] = partial.astype(IMAGE_WIRE)
        for s in range(1, cols):
            to = col_peer(s)
            n = (s - 1) * 2 + block
            copies.append(send(
                (p3 if IMAGE_WIRE == F32 else w3).at[block, rows_of(to)],
                r3.at[s - 1, block], s5.at[n], v5.at[n], at_col(to, k)))
    for copy in copies:
        copy.wait()
    for block in range(2):
        total = p3[block, own]
        for s in range(1, cols):
            total = total + r3[s - 1, block].astype(F32)
        x[k, block] = total
    pair = send(x.at[k], x.at[k], s6, v6, partner)
    pair.wait()
    im[c, k] = x[k, k]
    im[c, other] = x[other, k]

    mine = x[k].reshape(2 * part, width)
    grams = [
        lax.dot_general(x[j].reshape(2 * part, width), mine, (((0,), (0,)), ((), ())),
                        precision=HIGHEST, preferred_element_type=F32)
        for j in range(2)
    ]
    full = jnp.concatenate(grams, axis=0)
    piece = gp.shape[1]
    for to in range(cols):
        gp[to] = full[to * piece:(to + 1) * piece]
    copies = []
    for s in range(1, cols):
        to = col_peer(s)
        copies.append(send(gp.at[to], ra.at[s - 1], s7.at[s - 1], v7.at[s - 1], at_col(to, k)))
    images = []
    for s in range(1, cols):
        to = col_peer(s)
        images.append(send(x.at[k, k], im.at[c, k], s8.at[2 * s - 2], v8.at[2 * s - 2], at_col(to, k)))
        images.append(send(x.at[k, other], im.at[c, k], s8.at[2 * s - 1], v8.at[2 * s - 1], at_col(to, other)))
    for copy in copies:
        copy.wait()
    total = gp[c]
    for s in range(1, cols):
        total = total + ra[s - 1]
    gb[r] = total
    copies = []
    for s in range(1, groups):
        copies.append(send(gb.at[r], gb.at[r], s9.at[s - 1], v9.at[s - 1], at_row(row_peer(s))))
    for copy in copies:
        copy.wait()
    total = gb[0]
    for g in range(1, groups):
        total = total + gb[g]
    gf[k, c] = total
    copies = [send(gf.at[k, c], gf.at[k, c], load_sem.at[2], load_sem.at[3], partner)]
    n = 4
    for s in range(1, cols):
        for core in (k, other):
            copies.append(send(gf.at[k, c], gf.at[k, c], load_sem.at[n], load_sem.at[n + 1], at_col(col_peer(s), core)))
            n += 2
    for copy in copies:
        copy.wait()
    for copy in images:
        copy.wait()
    for core in range(2):
        for to in range(cols):
            gram_ref[to * piece:(to + 1) * piece, core * width:(core + 1) * width] = gf[core, to]
    for core in range(2):
        for to in range(cols):
            image_ref[to * part:(to + 1) * part, core * width:(core + 1) * width] = im[to, core]


def power_step(operator, test_matrix, sizes, ratio):
    outer, inner, cols = sizes
    rows, depth = operator.shape
    rank = test_matrix.shape[1]
    half = rank // 2
    groups = outer * inner // 2
    part = rows // cols
    lanes = half // groups
    dma = pltpu.SemaphoreType.DMA
    vmem = pltpu.VMEM
    blocks = (cols - 1, 2, part, half)
    tiny = (1, 8, 128)
    scratch = [
        vmem((2, rows, depth), BF16),
        vmem((depth, half), BF16),
        vmem((2, rows, half), F32),
        vmem((2, rows, half) if SKETCH_WIRE != F32 else tiny, SKETCH_WIRE),
        vmem(blocks, SKETCH_WIRE),
        vmem((2, rows, half), BF16),
        vmem((groups, lanes, depth), F32),
        vmem((groups, lanes, depth) if NORMAL_WIRE != F32 else tiny, NORMAL_WIRE),
        vmem((groups - 1, lanes, depth), NORMAL_WIRE),
        vmem((groups, lanes, depth), BF16),
        vmem((2, rows, half), F32),
        vmem((2, rows, half) if IMAGE_WIRE != F32 else tiny, IMAGE_WIRE),
        vmem(blocks, IMAGE_WIRE),
        vmem((2, 2, part, half), F32),
        vmem((cols, rank // cols, half), F32),
        vmem((cols - 1, rank // cols, half), F32),
        vmem((groups, rank // cols, half), F32),
        vmem((2, cols, rank // cols, half), F32),
        vmem((cols, 2, part, half), F32),
        dma((4 + 4 * (cols - 1),)),
        dma, dma,
    ]
    for count in (2 * (cols - 1), cols - 1, groups - 1, groups - 1, 2 * (cols - 1)):
        scratch += [dma((count,)), dma((count,))]
    scratch += [dma, dma]
    for count in (cols - 1, 2 * (cols - 1), groups - 1):
        scratch += [dma((count,)), dma((count,))]
    return pl.pallas_call(
        functools.partial(power_kernel, sizes, ratio),
        out_shape=(
            jax.ShapeDtypeStruct((rank, rank), F32),
            jax.ShapeDtypeStruct((rows, rank), F32),
        ),
        in_specs=[pl.BlockSpec(memory_space=pl.ANY)] * 2,
        out_specs=(pl.BlockSpec(memory_space=pltpu.VMEM),) * 2,
        scratch_shapes=scratch,
        compiler_params=pltpu.CompilerParams(
            collective_id=0, has_side_effects=True, vmem_limit_bytes=48 << 20
        ),
        name="power_step",
    )(operator, test_matrix)


def shards(operator, test_matrix):
    sizes = tuple(lax.axis_size(name) for name in ("outer", "inner", "col"))
    row_groups = sizes[0] * sizes[1]
    col_groups = sizes[2]
    total_rows = operator.shape[0] * row_groups
    total_cols = operator.shape[1] * col_groups
    gram, image = power_step(operator, test_matrix, sizes, total_cols / total_rows)
    lower = jnp.linalg.cholesky(gram)
    root = jnp.sqrt(jnp.float32(total_rows))
    width = image.shape[1] // col_groups
    orthonormal = jax.scipy.linalg.solve_triangular(lower, image.T, lower=True).T
    basis = lax.dynamic_slice_in_dim(orthonormal, lax.axis_index("col") * width, width, 1) * root
    factor = lower.T / root
    return (basis, factor)


def solution(mesh):
    placed = (P(("outer", "inner"), "col"), P("col", None))
    return jax.shard_map(
        shards,
        mesh=mesh,
        in_specs=placed,
        out_specs=(P(("outer", "inner"), "col"), P()),
        check_vma=False,
    )
```

```python
import functools

import jax
import jax.numpy as jnp
from jax import lax
from jax.experimental import pallas as pl
from jax.experimental.pallas import tpu as pltpu
from jax.sharding import PartitionSpec as P

F32 = jnp.float32
BF16 = jnp.bfloat16
MESH = pl.DeviceIdType.MESH
HIGHEST = lax.Precision.HIGHEST
SKETCH_WIRE = F32
NORMAL_WIRE = F32
IMAGE_WIRE = F32
BLOCK = 32


def power_kernel(
    sizes, ratio, a_hbm, om_hbm, gram_ref, image_ref,
    a, om, p1, w1, r1, sk, p2, w2, r2, nt, p3, w3, r3, x, gp, ra, gb, gf, im,
    load_sem, s0, v0, s1, v1, s2, v2, s3, v3, s4, v4, s5, v5, s6, v6, s7, v7, s8, v8, s9, v9,
):
    outer, inner, cols = sizes
    chips = inner // 2
    groups = outer * chips
    o, i, c = lax.axis_index("outer"), lax.axis_index("inner"), lax.axis_index("col")
    k = lax.rem(i, 2)
    other = 1 - k
    chip = lax.div(i, 2)
    r = o * chips + chip
    partner = (o, chip * 2 + other, c)

    def col_peer(s):
        return lax.rem(c + s, cols)

    def row_peer(s):
        return lax.rem(r + s, groups)

    def at_col(to, core):
        return (o, chip * 2 + core, to)

    def at_row(to):
        return (lax.div(to, chips), lax.rem(to, chips) * 2 + k, c)

    def send(src, dst, ss, rs, to):
        copy = pltpu.make_async_remote_copy(
            src_ref=src, dst_ref=dst, send_sem=ss, recv_sem=rs, device_id=to, device_id_type=MESH
        )
        copy.start()
        return copy

    load_a = pltpu.make_async_copy(a_hbm, a.at[k], load_sem.at[0])
    load_a.start()
    width = om.shape[1]
    load_om = pltpu.make_async_copy(
        om_hbm.at[:, pl.ds(pl.multiple_of(k * width, width), width)], om, load_sem.at[1]
    )
    load_om.start()

    barrier = pltpu.get_barrier_semaphore()
    peers = [partner]
    for s in range(1, cols):
        peers += [at_col(col_peer(s), k), at_col(col_peer(s), other)]
    for s in range(1, groups):
        peers.append(at_row(row_peer(s)))
    for to in peers:
        pl.semaphore_signal(barrier, inc=1, device_id=to, device_id_type=MESH)
    pl.semaphore_wait(barrier, len(peers))

    pair = send(a_hbm, a.at[k], s0, v0, partner)
    load_a.wait()
    load_om.wait()

    part = p1.shape[1] // cols
    own = pl.ds(pl.multiple_of(c * part, part), part)

    def rows_of(to):
        return pl.ds(pl.multiple_of(to * part, part), part)

    copies = []
    for turn, block in enumerate((k, other)):
        if turn == 1:
            pair.wait()
        partial = jnp.dot(a[block], om[...], preferred_element_type=F32)
        p1[block] = partial
        if SKETCH_WIRE != F32:
            w1[block] = partial.astype(SKETCH_WIRE)
        for s in range(1, cols):
            to = col_peer(s)
            n = (s - 1) * 2 + turn
            copies.append(send(
                (p1 if SKETCH_WIRE == F32 else w1).at[block, rows_of(to)],
                r1.at[s - 1, turn], s1.at[n], v1.at[n], at_col(to, k)))
    for copy in copies:
        copy.wait()
    for turn, block in enumerate((k, other)):
        total = p1[block, own]
        for s in range(1, cols):
            total = total + r1[s - 1, turn].astype(F32)
        sk[block, own] = total.astype(BF16)
    copies = []
    for s in range(1, cols):
        copies.append(send(sk.at[:, own], sk.at[:, own], s2.at[s - 1], v2.at[s - 1], at_col(col_peer(s), k)))
    for copy in copies:
        copy.wait()

    normal = None
    for block in range(2):
        st = sk[block].astype(F32).T.astype(BF16)
        term = jnp.dot(st, a[block], preferred_element_type=F32)
        normal = term if normal is None else normal + term
    lanes = p2.shape[1]
    for g in range(groups):
        p2[g] = normal[g * lanes:(g + 1) * lanes]
        if NORMAL_WIRE != F32:
            w2[g] = normal[g * lanes:(g + 1) * lanes].astype(NORMAL_WIRE)
    copies = []
    for s in range(1, groups):
        to = row_peer(s)
        copies.append(send((p2 if NORMAL_WIRE == F32 else w2).at[to], r2.at[s - 1], s3.at[s - 1], v3.at[s - 1], at_row(to)))
    for copy in copies:
        copy.wait()
    total = p2[r]
    for s in range(1, groups):
        total = total + r2[s - 1].astype(F32)
    nt[r] = (total * ratio).astype(BF16)
    copies = []
    for s in range(1, groups):
        copies.append(send(nt.at[r], nt.at[r], s4.at[s - 1], v4.at[s - 1], at_row(row_peer(s))))
    for copy in copies:
        copy.wait()
    if lanes % 16 == 0:
        whole = nt[...].reshape(groups * lanes, nt.shape[2])
    else:
        whole = jnp.concatenate([nt[g].astype(F32) for g in range(groups)], axis=0).astype(BF16)

    copies = []
    for block in range(2):
        partial = lax.dot_general(a[block], whole, (((1,), (1,)), ((), ())), preferred_element_type=F32)
        p3[block] = partial
        if IMAGE_WIRE != F32:
            w3[block] = partial.astype(IMAGE_WIRE)
        for s in range(1, cols):
            to = col_peer(s)
            n = (s - 1) * 2 + block
            copies.append(send(
                (p3 if IMAGE_WIRE == F32 else w3).at[block, rows_of(to)],
                r3.at[s - 1, block], s5.at[n], v5.at[n], at_col(to, k)))
    for copy in copies:
        copy.wait()
    for block in range(2):
        total = p3[block, own]
        for s in range(1, cols):
            total = total + r3[s - 1, block].astype(F32)
        x[k, block] = total
    pair = send(x.at[k], x.at[k], s6, v6, partner)
    pair.wait()
    im[c, k] = x[k, k]
    im[c, other] = x[other, k]

    mine = x[k].reshape(2 * part, width)
    grams = [
        lax.dot_general(x[j].reshape(2 * part, width), mine, (((0,), (0,)), ((), ())),
                        precision=HIGHEST, preferred_element_type=F32)
        for j in range(2)
    ]
    full = jnp.concatenate(grams, axis=0)
    piece = gp.shape[1]
    for to in range(cols):
        gp[to] = full[to * piece:(to + 1) * piece]
    copies = []
    for s in range(1, cols):
        to = col_peer(s)
        copies.append(send(gp.at[to], ra.at[s - 1], s7.at[s - 1], v7.at[s - 1], at_col(to, k)))
    images = []
    for s in range(1, cols):
        to = col_peer(s)
        images.append(send(x.at[k, k], im.at[c, k], s8.at[2 * s - 2], v8.at[2 * s - 2], at_col(to, k)))
        images.append(send(x.at[k, other], im.at[c, k], s8.at[2 * s - 1], v8.at[2 * s - 1], at_col(to, other)))
    for copy in copies:
        copy.wait()
    total = gp[c]
    for s in range(1, cols):
        total = total + ra[s - 1]
    gb[r] = total
    copies = []
    for s in range(1, groups):
        copies.append(send(gb.at[r], gb.at[r], s9.at[s - 1], v9.at[s - 1], at_row(row_peer(s))))
    for copy in copies:
        copy.wait()
    total = gb[0]
    for g in range(1, groups):
        total = total + gb[g]
    gf[k, c] = total
    copies = [send(gf.at[k, c], gf.at[k, c], load_sem.at[2], load_sem.at[3], partner)]
    n = 4
    for s in range(1, cols):
        for core in (k, other):
            copies.append(send(gf.at[k, c], gf.at[k, c], load_sem.at[n], load_sem.at[n + 1], at_col(col_peer(s), core)))
            n += 2
    for copy in copies:
        copy.wait()
    for copy in images:
        copy.wait()
    for core in range(2):
        for to in range(cols):
            gram_ref[to * piece:(to + 1) * piece, core * width:(core + 1) * width] = gf[core, to]
    for core in range(2):
        for to in range(cols):
            image_ref[to * part:(to + 1) * part, core * width:(core + 1) * width] = im[to, core]


def power_step(operator, test_matrix, sizes, ratio):
    outer, inner, cols = sizes
    rows, depth = operator.shape
    rank = test_matrix.shape[1]
    half = rank // 2
    groups = outer * inner // 2
    part = rows // cols
    lanes = half // groups
    dma = pltpu.SemaphoreType.DMA
    vmem = pltpu.VMEM
    blocks = (cols - 1, 2, part, half)
    tiny = (1, 8, 128)
    scratch = [
        vmem((2, rows, depth), BF16),
        vmem((depth, half), BF16),
        vmem((2, rows, half), F32),
        vmem((2, rows, half) if SKETCH_WIRE != F32 else tiny, SKETCH_WIRE),
        vmem(blocks, SKETCH_WIRE),
        vmem((2, rows, half), BF16),
        vmem((groups, lanes, depth), F32),
        vmem((groups, lanes, depth) if NORMAL_WIRE != F32 else tiny, NORMAL_WIRE),
        vmem((groups - 1, lanes, depth), NORMAL_WIRE),
        vmem((groups, lanes, depth), BF16),
        vmem((2, rows, half), F32),
        vmem((2, rows, half) if IMAGE_WIRE != F32 else tiny, IMAGE_WIRE),
        vmem(blocks, IMAGE_WIRE),
        vmem((2, 2, part, half), F32),
        vmem((cols, rank // cols, half), F32),
        vmem((cols - 1, rank // cols, half), F32),
        vmem((groups, rank // cols, half), F32),
        vmem((2, cols, rank // cols, half), F32),
        vmem((cols, 2, part, half), F32),
        dma((4 + 4 * (cols - 1),)),
        dma, dma,
    ]
    for count in (2 * (cols - 1), cols - 1, groups - 1, groups - 1, 2 * (cols - 1)):
        scratch += [dma((count,)), dma((count,))]
    scratch += [dma, dma]
    for count in (cols - 1, 2 * (cols - 1), groups - 1):
        scratch += [dma((count,)), dma((count,))]
    return pl.pallas_call(
        functools.partial(power_kernel, sizes, ratio),
        out_shape=(
            jax.ShapeDtypeStruct((rank, rank), F32),
            jax.ShapeDtypeStruct((rows, rank), F32),
        ),
        in_specs=[pl.BlockSpec(memory_space=pl.ANY)] * 2,
        out_specs=(pl.BlockSpec(memory_space=pltpu.VMEM),) * 2,
        scratch_shapes=scratch,
        compiler_params=pltpu.CompilerParams(
            collective_id=0, has_side_effects=True, vmem_limit_bytes=60 << 20
        ),
        name="power_step",
    )(operator, test_matrix)


def split(value):
    high = value.astype(BF16)
    rest = value - high.astype(F32)
    middle = rest.astype(BF16)
    low = (rest - middle.astype(F32)).astype(BF16)
    return high, middle, low


def factor_kernel(root, gram_ref, image_ref, basis_ref, factor_ref, s_ref, w_ref):
    size = gram_ref.shape[0]
    s_ref[...] = gram_ref[...]
    row = lax.broadcasted_iota(jnp.int32, (size, size), 0)
    col = lax.broadcasted_iota(jnp.int32, (size, size), 1)
    w_ref[...] = jnp.where(row == col, jnp.float32(1), jnp.float32(0))
    sub = lax.broadcasted_iota(jnp.int32, (8, 128), 0)
    wide = 128
    for start in range(0, size, BLOCK):
        rows = BLOCK // 8
        tiles = [(s_ref, t) for t in range(start // wide, size // wide)]
        tiles += [(w_ref, t) for t in range(0, start // wide + 1)]
        q = [[ref[start + 8 * g:start + 8 * g + 8, t * wide:(t + 1) * wide] for ref, t in tiles]
             for g in range(rows)]
        for p in range(rows):
            first = (start + 8 * p) % wide
            cs = [[jnp.broadcast_to(q[g][0][:, first + n:first + n + 1], (8, wide)) for n in range(8)]
                  for g in range(p, rows)]
            pivots = jnp.zeros((8, wide), F32)
            for n in range(8):
                pivot = jnp.broadcast_to(cs[0][n][n:n + 1], (8, wide))
                pivots = jnp.where(sub == n, pivot, pivots)
                inverse = 1.0 / pivot
                heads = {m: jnp.broadcast_to(cs[0][m][n:n + 1], (8, wide)) * inverse for m in range(n + 1, 8)}
                bodies = [jnp.broadcast_to(tile[n:n + 1], (8, wide)) * inverse for tile in q[p]]
                for g in range(p, rows):
                    weight = cs[g - p][n]
                    if g == p:
                        weight = jnp.where(sub > n, weight, 0.0)
                    for m in range(n + 1, 8):
                        cs[g - p][m] = cs[g - p][m] - weight * heads[m]
                    q[g] = [tile - weight * body for tile, body in zip(q[g], bodies)]
            scale = lax.rsqrt(pivots)
            q[p] = [tile * scale for tile in q[p]]
        for g in range(rows):
            for (ref, t), tile in zip(tiles, q[g]):
                ref[start + 8 * g:start + 8 * g + 8, t * wide:(t + 1) * wide] = tile
        done = start + BLOCK
        if done < size:
            block = jnp.concatenate([jnp.concatenate(q[g], axis=1) for g in range(rows)], axis=0)
            h, m, l = split(block)
            count = size // wide - start // wide
            base = (start // wide) * wide
            take = slice(done - base, count * wide) if (done - base) % wide == 0 else slice(0, count * wide)
            skip = done - base - (take.start or 0)
            left = jnp.concatenate([h, h, m, m, h, l], axis=0)[:, take]
            right = jnp.concatenate([h, m, h, m, l, h], axis=0)
            update = lax.dot_general(left, right, (((0,), (0,)), ((), ())), preferred_element_type=F32)[skip:]
            for at, (ref, t) in enumerate(tiles):
                lanes = slice(t * wide, (t + 1) * wide)
                ref[done:, lanes] = ref[done:, lanes] - update[:, at * wide:(at + 1) * wide]
    factor_ref[...] = jnp.where(row <= col, s_ref[...], 0.0) / root
    width = basis_ref.shape[1]
    mine = pl.ds(pl.multiple_of(lax.axis_index("col") * width, width), width)
    basis_ref[...] = lax.dot_general(
        image_ref[...], w_ref[mine, :], (((1,), (1,)), ((), ())),
        precision=HIGHEST, preferred_element_type=F32) * root


def factor_step(gram, image, root, width):
    size = gram.shape[0]
    vmem = pl.BlockSpec(memory_space=pltpu.VMEM)
    return pl.pallas_call(
        functools.partial(factor_kernel, root),
        out_shape=(
            jax.ShapeDtypeStruct((image.shape[0], width), F32),
            jax.ShapeDtypeStruct(gram.shape, F32),
        ),
        in_specs=[vmem, vmem],
        out_specs=(vmem, vmem),
        scratch_shapes=[pltpu.VMEM((size, size), F32), pltpu.VMEM((size, size), F32)],
        name="factor_step",
    )(gram, image)


def shards(operator, test_matrix):
    sizes = tuple(lax.axis_size(name) for name in ("outer", "inner", "col"))
    row_groups = sizes[0] * sizes[1]
    col_groups = sizes[2]
    total_rows = operator.shape[0] * row_groups
    total_cols = operator.shape[1] * col_groups
    gram, image = power_step(operator, test_matrix, sizes, total_cols / total_rows)
    root = float(total_rows) ** 0.5
    basis, factor = factor_step(gram, image, root, image.shape[1] // col_groups)
    return (basis, factor)


def solution(mesh):
    placed = (P(("outer", "inner"), "col"), P("col", None))
    return jax.shard_map(
        shards,
        mesh=mesh,
        in_specs=placed,
        out_specs=(P(("outer", "inner"), "col"), P()),
        check_vma=False,
    )
```

```python
import functools

import jax
import jax.numpy as jnp
from jax import lax
from jax.experimental import pallas as pl
from jax.experimental.pallas import tpu as pltpu
from jax.sharding import PartitionSpec as P

F32 = jnp.float32
BF16 = jnp.bfloat16
MESH = pl.DeviceIdType.MESH
HIGHEST = lax.Precision.HIGHEST
SKETCH_WIRE = F32
NORMAL_WIRE = BF16
IMAGE_WIRE = BF16
BLOCK = 32


def split(value):
    high = value.astype(BF16)
    rest = value - high.astype(F32)
    middle = rest.astype(BF16)
    low = (rest - middle.astype(F32)).astype(BF16)
    return high, middle, low


def eliminate(s_ref, w_ref):
    size = s_ref.shape[0]
    row = lax.broadcasted_iota(jnp.int32, (size, size), 0)
    col = lax.broadcasted_iota(jnp.int32, (size, size), 1)
    w_ref[...] = jnp.where(row == col, jnp.float32(1), jnp.float32(0))
    sub = lax.broadcasted_iota(jnp.int32, (8, 128), 0)
    wide = 128
    for start in range(0, size, BLOCK):
        rows = BLOCK // 8
        tiles = [(s_ref, t) for t in range(start // wide, size // wide)]
        tiles += [(w_ref, t) for t in range(0, start // wide + 1)]
        q = [[ref[start + 8 * g:start + 8 * g + 8, t * wide:(t + 1) * wide] for ref, t in tiles]
             for g in range(rows)]
        for p in range(rows):
            first = (start + 8 * p) % wide
            cs = [[jnp.broadcast_to(q[g][0][:, first + n:first + n + 1], (8, wide)) for n in range(8)]
                  for g in range(p, rows)]
            pivots = jnp.zeros((8, wide), F32)
            for n in range(8):
                pivot = jnp.broadcast_to(cs[0][n][n:n + 1], (8, wide))
                pivots = jnp.where(sub == n, pivot, pivots)
                inverse = 1.0 / pivot
                heads = {m: jnp.broadcast_to(cs[0][m][n:n + 1], (8, wide)) * inverse for m in range(n + 1, 8)}
                bodies = [jnp.broadcast_to(tile[n:n + 1], (8, wide)) * inverse for tile in q[p]]
                for g in range(p, rows):
                    weight = cs[g - p][n]
                    if g == p:
                        weight = jnp.where(sub > n, weight, 0.0)
                    for m in range(n + 1, 8):
                        cs[g - p][m] = cs[g - p][m] - weight * heads[m]
                    q[g] = [tile - weight * body for tile, body in zip(q[g], bodies)]
            scale = lax.rsqrt(pivots)
            q[p] = [tile * scale for tile in q[p]]
        for g in range(rows):
            for (ref, t), tile in zip(tiles, q[g]):
                ref[start + 8 * g:start + 8 * g + 8, t * wide:(t + 1) * wide] = tile
        done = start + BLOCK
        if done < size:
            block = jnp.concatenate([jnp.concatenate(q[g], axis=1) for g in range(rows)], axis=0)
            h, m, l = split(block)
            count = size // wide - start // wide
            base = (start // wide) * wide
            take = slice(done - base, count * wide) if (done - base) % wide == 0 else slice(0, count * wide)
            skip = done - base - (take.start or 0)
            left = jnp.concatenate([h, h, m, m, h, l], axis=0)[:, take]
            right = jnp.concatenate([h, m, h, m, l, h], axis=0)
            update = lax.dot_general(left, right, (((0,), (0,)), ((), ())), preferred_element_type=F32)[skip:]
            for at, (ref, t) in enumerate(tiles):
                lanes = slice(t * wide, (t + 1) * wide)
                ref[done:, lanes] = ref[done:, lanes] - update[:, at * wide:(at + 1) * wide]


def power_kernel(
    sizes, ratio, root, a_hbm, om_hbm, basis_ref, factor_ref,
    a, om, p1, w1, r1, sk, p2, w2, r2, nt, p3, w3, r3, x, gp, ra, gb, gf, im, s_ref, w_ref,
    load_sem, s0, v0, s1, v1, s2, v2, s3, v3, s4, v4, s5, v5, s6, v6, s7, v7, s8, v8, s9, v9,
):
    outer, inner, cols = sizes
    chips = inner // 2
    groups = outer * chips
    o, i, c = lax.axis_index("outer"), lax.axis_index("inner"), lax.axis_index("col")
    k = lax.rem(i, 2)
    other = 1 - k
    chip = lax.div(i, 2)
    r = o * chips + chip
    partner = (o, chip * 2 + other, c)

    def col_peer(s):
        return lax.rem(c + s, cols)

    def row_peer(s):
        return lax.rem(r + s, groups)

    def at_col(to, core):
        return (o, chip * 2 + core, to)

    def at_row(to, core):
        return (lax.div(to, chips), lax.rem(to, chips) * 2 + core, c)

    def send(src, dst, ss, rs, to):
        copy = pltpu.make_async_remote_copy(
            src_ref=src, dst_ref=dst, send_sem=ss, recv_sem=rs, device_id=to, device_id_type=MESH
        )
        copy.start()
        return copy

    load_a = pltpu.make_async_copy(a_hbm, a.at[k], load_sem.at[0])
    load_a.start()
    width = om.shape[1]
    load_om = pltpu.make_async_copy(
        om_hbm.at[:, pl.ds(pl.multiple_of(k * width, width), width)], om, load_sem.at[1]
    )
    load_om.start()

    barrier = pltpu.get_barrier_semaphore()
    peers = [partner]
    for s in range(1, cols):
        peers += [at_col(col_peer(s), k), at_col(col_peer(s), other)]
    for s in range(1, groups):
        peers += [at_row(row_peer(s), k), at_row(row_peer(s), other)]
    for to in peers:
        pl.semaphore_signal(barrier, inc=1, device_id=to, device_id_type=MESH)
    pl.semaphore_wait(barrier, len(peers))

    pair = send(a_hbm, a.at[k], s0, v0, partner)
    load_a.wait()
    load_om.wait()

    part = p1.shape[1] // cols
    own = pl.ds(pl.multiple_of(c * part, part), part)

    def rows_of(to):
        return pl.ds(pl.multiple_of(to * part, part), part)

    copies = []
    for turn, block in enumerate((k, other)):
        if turn == 1:
            pair.wait()
        partial = jnp.dot(a[block], om[...], preferred_element_type=F32)
        p1[block] = partial
        if SKETCH_WIRE != F32:
            w1[block] = partial.astype(SKETCH_WIRE)
        for s in range(1, cols):
            to = col_peer(s)
            n = (s - 1) * 2 + turn
            copies.append(send(
                (p1 if SKETCH_WIRE == F32 else w1).at[block, rows_of(to)],
                r1.at[s - 1, turn], s1.at[n], v1.at[n], at_col(to, k)))
    for copy in copies:
        copy.wait()
    for turn, block in enumerate((k, other)):
        total = p1[block, own]
        for s in range(1, cols):
            total = total + r1[s - 1, turn].astype(F32)
        sk[block, own] = total.astype(BF16)
    copies = []
    for s in range(1, cols):
        copies.append(send(sk.at[:, own], sk.at[:, own], s2.at[s - 1], v2.at[s - 1], at_col(col_peer(s), k)))
    for copy in copies:
        copy.wait()

    normal = None
    for block in range(2):
        st = sk[block].astype(F32).T.astype(BF16)
        term = jnp.dot(st, a[block], preferred_element_type=F32)
        normal = term if normal is None else normal + term
    lanes = p2.shape[1]
    for g in range(groups):
        p2[g] = normal[g * lanes:(g + 1) * lanes]
        if NORMAL_WIRE != F32:
            w2[g] = normal[g * lanes:(g + 1) * lanes].astype(NORMAL_WIRE)
    copies = []
    for s in range(1, groups):
        to = row_peer(s)
        copies.append(send((p2 if NORMAL_WIRE == F32 else w2).at[to], r2.at[s - 1], s3.at[s - 1], v3.at[s - 1], at_row(to, k)))
    for copy in copies:
        copy.wait()
    total = p2[r]
    for s in range(1, groups):
        total = total + r2[s - 1].astype(F32)
    nt[r] = (total * ratio).astype(BF16)
    copies = []
    for s in range(1, groups):
        copies.append(send(nt.at[r], nt.at[r], s4.at[s - 1], v4.at[s - 1], at_row(row_peer(s), k)))
    for copy in copies:
        copy.wait()
    if lanes % 16 == 0:
        whole = nt[...].reshape(groups * lanes, nt.shape[2])
    else:
        whole = jnp.concatenate([nt[g].astype(F32) for g in range(groups)], axis=0).astype(BF16)

    copies = []
    for block in range(2):
        partial = lax.dot_general(a[block], whole, (((1,), (1,)), ((), ())), preferred_element_type=F32)
        p3[block] = partial
        if IMAGE_WIRE != F32:
            w3[block] = partial.astype(IMAGE_WIRE)
        for s in range(1, cols):
            to = col_peer(s)
            n = (s - 1) * 2 + block
            copies.append(send(
                (p3 if IMAGE_WIRE == F32 else w3).at[block, rows_of(to)],
                r3.at[s - 1, block], s5.at[n], v5.at[n], at_col(to, k)))
    for copy in copies:
        copy.wait()
    for block in range(2):
        total = p3[block, own]
        for s in range(1, cols):
            total = total + r3[s - 1, block].astype(F32)
        x[k, block] = total
    pair = send(x.at[k], x.at[k], s6, v6, partner)
    pair.wait()
    im[c, k] = x[k, k]
    im[c, other] = x[other, k]

    mine = x[k].reshape(2 * part, width)
    grams = [
        lax.dot_general(x[j].reshape(2 * part, width), mine, (((0,), (0,)), ((), ())),
                        precision=HIGHEST, preferred_element_type=F32)
        for j in range(2)
    ]
    full = jnp.concatenate(grams, axis=0)
    piece = gp.shape[1]
    for to in range(groups):
        gp[to] = full[to * piece:(to + 1) * piece]
    copies = []
    for s in range(1, groups):
        to = row_peer(s)
        copies.append(send(gp.at[to], ra.at[s - 1], s7.at[s - 1], v7.at[s - 1], at_row(to, k)))
    for copy in copies:
        copy.wait()
    total = gp[r]
    for s in range(1, groups):
        total = total + ra[s - 1]
    gb[c] = total
    copies = []
    for s in range(1, cols):
        copies.append(send(gb.at[c], gb.at[c], s9.at[s - 1], v9.at[s - 1], at_col(col_peer(s), k)))
    images = []
    for s in range(1, cols):
        to = col_peer(s)
        images.append(send(x.at[k, k], im.at[c, k], s8.at[2 * s - 2], v8.at[2 * s - 2], at_col(to, k)))
        images.append(send(x.at[k, other], im.at[c, k], s8.at[2 * s - 1], v8.at[2 * s - 1], at_col(to, other)))
    for copy in copies:
        copy.wait()
    total = gb[0]
    for to in range(1, cols):
        total = total + gb[to]
    gf[k, r] = total
    copies = [send(gf.at[k, r], gf.at[k, r], load_sem.at[2], load_sem.at[3], partner)]
    n = 4
    for s in range(1, groups):
        for core in (k, other):
            copies.append(send(gf.at[k, r], gf.at[k, r], load_sem.at[n], load_sem.at[n + 1], at_row(row_peer(s), core)))
            n += 2
    for copy in copies:
        copy.wait()
    for core in range(2):
        for g in range(groups):
            s_ref[g * piece:(g + 1) * piece, core * width:(core + 1) * width] = gf[core, g]
    eliminate(s_ref, w_ref)
    size = s_ref.shape[0]
    row = lax.broadcasted_iota(jnp.int32, (size, size), 0)
    col = lax.broadcasted_iota(jnp.int32, (size, size), 1)
    factor_ref[...] = jnp.where(row <= col, s_ref[...], 0.0) / root
    columns = basis_ref.shape[0]
    inverse = w_ref[pl.ds(pl.multiple_of(c * columns, columns), columns), :]
    for copy in images:
        copy.wait()
    for to in range(cols):
        total = None
        for core in range(2):
            term = lax.dot_general(
                inverse[:, core * width:(core + 1) * width], im[to, core], (((1,), (1,)), ((), ())),
                precision=HIGHEST, preferred_element_type=F32)
            total = term if total is None else total + term
        basis_ref[:, to * part:(to + 1) * part] = total * root


def power_step(operator, test_matrix, sizes, ratio, root):
    outer, inner, cols = sizes
    rows, depth = operator.shape
    rank = test_matrix.shape[1]
    half = rank // 2
    groups = outer * inner // 2
    part = rows // cols
    lanes = half // groups
    dma = pltpu.SemaphoreType.DMA
    vmem = pltpu.VMEM
    blocks = (cols - 1, 2, part, half)
    tiny = (1, 8, 128)
    scratch = [
        vmem((2, rows, depth), BF16),
        vmem((depth, half), BF16),
        vmem((2, rows, half), F32),
        vmem((2, rows, half) if SKETCH_WIRE != F32 else tiny, SKETCH_WIRE),
        vmem(blocks, SKETCH_WIRE),
        vmem((2, rows, half), BF16),
        vmem((groups, lanes, depth), F32),
        vmem((groups, lanes, depth) if NORMAL_WIRE != F32 else tiny, NORMAL_WIRE),
        vmem((groups - 1, lanes, depth), NORMAL_WIRE),
        vmem((groups, lanes, depth), BF16),
        vmem((2, rows, half), F32),
        vmem((2, rows, half) if IMAGE_WIRE != F32 else tiny, IMAGE_WIRE),
        vmem(blocks, IMAGE_WIRE),
        vmem((2, 2, part, half), F32),
        vmem((groups, rank // groups, half), F32),
        vmem((groups - 1, rank // groups, half), F32),
        vmem((cols, rank // groups, half), F32),
        vmem((2, groups, rank // groups, half), F32),
        vmem((cols, 2, part, half), F32),
        vmem((rank, rank), F32),
        vmem((rank, rank), F32),
        dma((4 + 4 * (groups - 1),)),
        dma, dma,
    ]
    for count in (2 * (cols - 1), cols - 1, groups - 1, groups - 1, 2 * (cols - 1)):
        scratch += [dma((count,)), dma((count,))]
    scratch += [dma, dma]
    for count in (groups - 1, 2 * (cols - 1), cols - 1):
        scratch += [dma((count,)), dma((count,))]
    return pl.pallas_call(
        functools.partial(power_kernel, sizes, ratio, root),
        out_shape=(
            jax.ShapeDtypeStruct((rank // cols, rows), F32),
            jax.ShapeDtypeStruct((rank, rank), F32),
        ),
        in_specs=[pl.BlockSpec(memory_space=pl.ANY)] * 2,
        out_specs=(pl.BlockSpec(memory_space=pltpu.VMEM),) * 2,
        scratch_shapes=scratch,
        compiler_params=pltpu.CompilerParams(
            collective_id=0, has_side_effects=True, vmem_limit_bytes=60 << 20
        ),
        name="power_step",
    )(operator, test_matrix)


def shards(operator, test_matrix):
    sizes = tuple(lax.axis_size(name) for name in ("outer", "inner", "col"))
    row_groups = sizes[0] * sizes[1]
    col_groups = sizes[2]
    total_rows = operator.shape[0] * row_groups
    total_cols = operator.shape[1] * col_groups
    root = float(total_rows) ** 0.5
    basis, factor = power_step(operator, test_matrix, sizes, total_cols / total_rows, root)
    return (basis.T, factor)


def solution(mesh):
    placed = (P(("outer", "inner"), "col"), P("col", None))
    return jax.shard_map(
        shards,
        mesh=mesh,
        in_specs=placed,
        out_specs=(P(("outer", "inner"), "col"), P()),
        check_vma=False,
    )
```

```python
import functools

import jax
import jax.numpy as jnp
from jax import lax
from jax.experimental import pallas as pl
from jax.experimental.pallas import tpu as pltpu
from jax.sharding import PartitionSpec as P

F32 = jnp.float32
BF16 = jnp.bfloat16
MESH = pl.DeviceIdType.MESH
HIGHEST = lax.Precision.HIGHEST
SPANS = 2
NORMAL_WIRE = BF16
IMAGE_WIRE = BF16
BLOCK = 32


def split(value):
    high = value.astype(BF16)
    rest = value - high.astype(F32)
    middle = rest.astype(BF16)
    low = (rest - middle.astype(F32)).astype(BF16)
    return high, middle, low


def eliminate(s_ref, w_ref):
    size = s_ref.shape[0]
    row = lax.broadcasted_iota(jnp.int32, (size, size), 0)
    col = lax.broadcasted_iota(jnp.int32, (size, size), 1)
    w_ref[...] = jnp.where(row == col, jnp.float32(1), jnp.float32(0))
    sub = lax.broadcasted_iota(jnp.int32, (8, 128), 0)
    wide = 128
    for start in range(0, size, BLOCK):
        rows = BLOCK // 8
        tiles = [(s_ref, t) for t in range(start // wide, size // wide)]
        tiles += [(w_ref, t) for t in range(0, start // wide + 1)]
        q = [[ref[start + 8 * g:start + 8 * g + 8, t * wide:(t + 1) * wide] for ref, t in tiles]
             for g in range(rows)]
        for p in range(rows):
            first = (start + 8 * p) % wide
            cs = [[jnp.broadcast_to(q[g][0][:, first + n:first + n + 1], (8, wide)) for n in range(8)]
                  for g in range(p, rows)]
            pivots = jnp.zeros((8, wide), F32)
            for n in range(8):
                pivot = jnp.broadcast_to(cs[0][n][n:n + 1], (8, wide))
                pivots = jnp.where(sub == n, pivot, pivots)
                inverse = 1.0 / pivot
                heads = {m: jnp.broadcast_to(cs[0][m][n:n + 1], (8, wide)) * inverse for m in range(n + 1, 8)}
                bodies = [jnp.broadcast_to(tile[n:n + 1], (8, wide)) * inverse for tile in q[p]]
                for g in range(p, rows):
                    weight = cs[g - p][n]
                    if g == p:
                        weight = jnp.where(sub > n, weight, 0.0)
                    for m in range(n + 1, 8):
                        cs[g - p][m] = cs[g - p][m] - weight * heads[m]
                    q[g] = [tile - weight * body for tile, body in zip(q[g], bodies)]
            scale = lax.rsqrt(pivots)
            q[p] = [tile * scale for tile in q[p]]
        for g in range(rows):
            for (ref, t), tile in zip(tiles, q[g]):
                ref[start + 8 * g:start + 8 * g + 8, t * wide:(t + 1) * wide] = tile
        done = start + BLOCK
        if done < size:
            block = jnp.concatenate([jnp.concatenate(q[g], axis=1) for g in range(rows)], axis=0)
            h, m, l = split(block)
            count = size // wide - start // wide
            base = (start // wide) * wide
            take = slice(done - base, count * wide) if (done - base) % wide == 0 else slice(0, count * wide)
            skip = done - base - (take.start or 0)
            left = jnp.concatenate([h, h, m, m, h, l], axis=0)[:, take]
            right = jnp.concatenate([h, m, h, m, l, h], axis=0)
            update = lax.dot_general(left, right, (((0,), (0,)), ((), ())), preferred_element_type=F32)[skip:]
            for at, (ref, t) in enumerate(tiles):
                lanes = slice(t * wide, (t + 1) * wide)
                ref[done:, lanes] = ref[done:, lanes] - update[:, at * wide:(at + 1) * wide]


def power_kernel(
    sizes, ratio, root, a_hbm, om_hbm, basis_ref, factor_ref,
    a, om, p1, r1, sk, p2, w2, r2, nt, p3, w3, r3, x, gp, ra, gb, gf, im, s_ref, w_ref,
    load_sem, s0, v0, s1, v1, s2, v2, s3, v3, s4, v4, s5, v5, s6, v6, s7, v7, s8, v8, s9, v9,
):
    outer, inner, cols = sizes
    chips = inner // 2
    groups = outer * chips
    o, i, c = lax.axis_index("outer"), lax.axis_index("inner"), lax.axis_index("col")
    k = lax.rem(i, 2)
    other = 1 - k
    chip = lax.div(i, 2)
    r = o * chips + chip
    partner = (o, chip * 2 + other, c)

    def col_peer(s):
        return lax.rem(c + s, cols)

    def row_peer(s):
        return lax.rem(r + s, groups)

    def at_col(to, core):
        return (o, chip * 2 + core, to)

    def at_row(to, core):
        return (lax.div(to, chips), lax.rem(to, chips) * 2 + core, c)

    def send(src, dst, ss, rs, to):
        copy = pltpu.make_async_remote_copy(
            src_ref=src, dst_ref=dst, send_sem=ss, recv_sem=rs, device_id=to, device_id_type=MESH
        )
        copy.start()
        return copy

    load_a = pltpu.make_async_copy(a_hbm, a.at[k], load_sem.at[0])
    load_a.start()
    width = om.shape[1]
    load_om = pltpu.make_async_copy(
        om_hbm.at[:, pl.ds(pl.multiple_of(k * width, width), width)], om, load_sem.at[1]
    )
    load_om.start()

    barrier = pltpu.get_barrier_semaphore()
    peers = [partner]
    for s in range(1, cols):
        peers += [at_col(col_peer(s), k), at_col(col_peer(s), other)]
    for s in range(1, groups):
        peers += [at_row(row_peer(s), k), at_row(row_peer(s), other)]
    for to in peers:
        pl.semaphore_signal(barrier, inc=1, device_id=to, device_id_type=MESH)
    load_a.wait()
    load_om.wait()
    p1[k] = jnp.dot(a[k], om[...], preferred_element_type=F32)
    pl.semaphore_wait(barrier, len(peers))
    pair = send(a_hbm, a.at[k], s0, v0, partner)

    part = p1.shape[1] // cols
    own = pl.ds(pl.multiple_of(c * part, part), part)

    def rows_of(to):
        return pl.ds(pl.multiple_of(to * part, part), part)

    sums = []
    for turn, block in enumerate((k, other)):
        if turn == 1:
            pair.wait()
            p1[block] = jnp.dot(a[block], om[...], preferred_element_type=F32)
        copies = []
        for s in range(1, cols):
            to = col_peer(s)
            n = (s - 1) * 2 + turn
            copies.append(send(p1.at[block, rows_of(to)], r1.at[s - 1, turn], s1.at[n], v1.at[n], at_col(to, k)))
        sums.append(copies)
    wholes = []
    for turn, block in enumerate((k, other)):
        for copy in sums[turn]:
            copy.wait()
        total = p1[block, own]
        for s in range(1, cols):
            total = total + r1[s - 1, turn].astype(F32)
        sk[block, own] = total.astype(BF16)
        copies = []
        for s in range(1, cols):
            n = (s - 1) * 2 + turn
            copies.append(send(sk.at[block, own], sk.at[block, own], s2.at[n], v2.at[n], at_col(col_peer(s), k)))
        wholes.append(copies)

    turned = []
    for turn, block in enumerate((k, other)):
        for copy in wholes[turn]:
            copy.wait()
        turned.append(sk[block].astype(F32).T.astype(BF16))
    lanes = p2.shape[2]
    depth = p2.shape[3]
    sums = []
    for span in range(SPANS):
        at = slice(span * depth, (span + 1) * depth)
        normal = None
        for st, block in zip(turned, (k, other)):
            term = jnp.dot(st, a[block, :, at], preferred_element_type=F32)
            normal = term if normal is None else normal + term
        for g in range(groups):
            p2[span, g] = normal[g * lanes:(g + 1) * lanes]
            w2[span, g] = normal[g * lanes:(g + 1) * lanes].astype(NORMAL_WIRE)
        copies = []
        for s in range(1, groups):
            to = row_peer(s)
            copies.append(send(w2.at[span, to], r2.at[span, s - 1], s3.at[span, s - 1], v3.at[span, s - 1], at_row(to, k)))
        sums.append(copies)
    wholes = []
    for span in range(SPANS):
        for copy in sums[span]:
            copy.wait()
        total = p2[span, r]
        for s in range(1, groups):
            total = total + r2[span, s - 1].astype(F32)
        nt[span, r] = (total * ratio).astype(BF16)
        copies = []
        for s in range(1, groups):
            copies.append(send(nt.at[span, r], nt.at[span, r], s4.at[span, s - 1], v4.at[span, s - 1], at_row(row_peer(s), k)))
        wholes.append(copies)

    copies = []
    spans = []
    for span in range(SPANS):
        for copy in wholes[span]:
            copy.wait()
        if lanes % 16 == 0:
            spans.append(nt[span].reshape(groups * lanes, depth))
        else:
            spans.append(jnp.concatenate([nt[span, g].astype(F32) for g in range(groups)], axis=0).astype(BF16))
        if span < SPANS - 1:
            for block in range(2):
                term = lax.dot_general(a[block, :, span * depth:(span + 1) * depth], spans[span],
                                       (((1,), (1,)), ((), ())), preferred_element_type=F32)
                p3[block] = term if span == 0 else p3[block] + term
    for block in range(2):
        partial = lax.dot_general(a[block, :, (SPANS - 1) * depth:], spans[-1],
                                  (((1,), (1,)), ((), ())), preferred_element_type=F32)
        if SPANS > 1:
            partial = p3[block] + partial
        p3[block] = partial
        w3[block] = partial.astype(IMAGE_WIRE)
        for s in range(1, cols):
            to = col_peer(s)
            n = (s - 1) * 2 + block
            copies.append(send(
                w3.at[block, rows_of(to)],
                r3.at[s - 1, block], s5.at[n], v5.at[n], at_col(to, k)))
    for copy in copies:
        copy.wait()
    for block in range(2):
        total = p3[block, own]
        for s in range(1, cols):
            total = total + r3[s - 1, block].astype(F32)
        x[k, block] = total
    pair = send(x.at[k], x.at[k], s6, v6, partner)
    pair.wait()
    im[c, k] = x[k, k]
    im[c, other] = x[other, k]

    mine = x[k].reshape(2 * part, width)
    grams = [
        lax.dot_general(x[j].reshape(2 * part, width), mine, (((0,), (0,)), ((), ())),
                        precision=HIGHEST, preferred_element_type=F32)
        for j in range(2)
    ]
    full = jnp.concatenate(grams, axis=0)
    piece = gp.shape[1]
    for to in range(groups):
        gp[to] = full[to * piece:(to + 1) * piece]
    copies = []
    for s in range(1, groups):
        to = row_peer(s)
        copies.append(send(gp.at[to], ra.at[s - 1], s7.at[s - 1], v7.at[s - 1], at_row(to, k)))
    for copy in copies:
        copy.wait()
    total = gp[r]
    for s in range(1, groups):
        total = total + ra[s - 1]
    gb[c] = total
    copies = []
    for s in range(1, cols):
        copies.append(send(gb.at[c], gb.at[c], s9.at[s - 1], v9.at[s - 1], at_col(col_peer(s), k)))
    images = []
    for s in range(1, cols):
        to = col_peer(s)
        images.append(send(x.at[k, k], im.at[c, k], s8.at[2 * s - 2], v8.at[2 * s - 2], at_col(to, k)))
        images.append(send(x.at[k, other], im.at[c, k], s8.at[2 * s - 1], v8.at[2 * s - 1], at_col(to, other)))
    for copy in copies:
        copy.wait()
    total = gb[0]
    for to in range(1, cols):
        total = total + gb[to]
    gf[k, r] = total
    copies = [send(gf.at[k, r], gf.at[k, r], load_sem.at[2], load_sem.at[3], partner)]
    n = 4
    for s in range(1, groups):
        for core in (k, other):
            copies.append(send(gf.at[k, r], gf.at[k, r], load_sem.at[n], load_sem.at[n + 1], at_row(row_peer(s), core)))
            n += 2
    for copy in copies:
        copy.wait()
    for core in range(2):
        for g in range(groups):
            s_ref[g * piece:(g + 1) * piece, core * width:(core + 1) * width] = gf[core, g]
    eliminate(s_ref, w_ref)
    size = s_ref.shape[0]
    row = lax.broadcasted_iota(jnp.int32, (size, size), 0)
    col = lax.broadcasted_iota(jnp.int32, (size, size), 1)
    factor_ref[...] = jnp.where(row <= col, s_ref[...], 0.0) / root
    columns = basis_ref.shape[0]
    inverse = w_ref[pl.ds(pl.multiple_of(c * columns, columns), columns), :]
    for copy in images:
        copy.wait()
    for to in range(cols):
        total = None
        for core in range(2):
            term = lax.dot_general(
                inverse[:, core * width:(core + 1) * width], im[to, core], (((1,), (1,)), ((), ())),
                precision=HIGHEST, preferred_element_type=F32)
            total = term if total is None else total + term
        basis_ref[:, to * part:(to + 1) * part] = total * root


def power_step(operator, test_matrix, sizes, ratio, root):
    outer, inner, cols = sizes
    rows, depth = operator.shape
    rank = test_matrix.shape[1]
    half = rank // 2
    groups = outer * inner // 2
    part = rows // cols
    lanes = half // groups
    dma = pltpu.SemaphoreType.DMA
    vmem = pltpu.VMEM
    blocks = (cols - 1, 2, part, half)
    span = depth // SPANS
    scratch = [
        vmem((2, rows, depth), BF16),
        vmem((depth, half), BF16),
        vmem((2, rows, half), F32),
        vmem(blocks, F32),
        vmem((2, rows, half), BF16),
        vmem((SPANS, groups, lanes, span), F32),
        vmem((SPANS, groups, lanes, span), NORMAL_WIRE),
        vmem((SPANS, groups - 1, lanes, span), NORMAL_WIRE),
        vmem((SPANS, groups, lanes, span), BF16),
        vmem((2, rows, half), F32),
        vmem((2, rows, half), IMAGE_WIRE),
        vmem(blocks, IMAGE_WIRE),
        vmem((2, 2, part, half), F32),
        vmem((groups, rank // groups, half), F32),
        vmem((groups - 1, rank // groups, half), F32),
        vmem((cols, rank // groups, half), F32),
        vmem((2, groups, rank // groups, half), F32),
        vmem((cols, 2, part, half), F32),
        vmem((rank, rank), F32),
        vmem((rank, rank), F32),
        dma((4 + 4 * (groups - 1),)),
        dma, dma,
    ]
    across, along = (2 * (cols - 1),), (SPANS, groups - 1)
    for shape in (across, across, along, along, across):
        scratch += [dma(shape), dma(shape)]
    scratch += [dma, dma]
    for count in (groups - 1, 2 * (cols - 1), cols - 1):
        scratch += [dma((count,)), dma((count,))]
    return pl.pallas_call(
        functools.partial(power_kernel, sizes, ratio, root),
        out_shape=(
            jax.ShapeDtypeStruct((rank // cols, rows), F32),
            jax.ShapeDtypeStruct((rank, rank), F32),
        ),
        in_specs=[pl.BlockSpec(memory_space=pl.ANY)] * 2,
        out_specs=(pl.BlockSpec(memory_space=pltpu.VMEM),) * 2,
        scratch_shapes=scratch,
        compiler_params=pltpu.CompilerParams(
            collective_id=0, has_side_effects=True, vmem_limit_bytes=60 << 20
        ),
        name="power_step",
    )(operator, test_matrix)


def shards(operator, test_matrix):
    sizes = tuple(lax.axis_size(name) for name in ("outer", "inner", "col"))
    row_groups = sizes[0] * sizes[1]
    col_groups = sizes[2]
    total_rows = operator.shape[0] * row_groups
    total_cols = operator.shape[1] * col_groups
    root = float(total_rows) ** 0.5
    basis, factor = power_step(operator, test_matrix, sizes, total_cols / total_rows, root)
    return (basis.T, factor)


def solution(mesh):
    placed = (P(("outer", "inner"), "col"), P("col", None))
    return jax.shard_map(
        shards,
        mesh=mesh,
        in_specs=placed,
        out_specs=(P(("outer", "inner"), "col"), P()),
        check_vma=False,
    )
```
